256 devices in a mesh: dp: 16 (over y_hi, x, core), seq: 16 (over y_lo, z).
Axes of the slice: x: 4, y: 4 (y_hi: 2, y_lo: 2; y = y_hi * 2 + y_lo), z: 8, core: 2. Of those that a mesh axis runs over, the one named last changes fastest.
Arguments:
- queries: bfloat16 [16, 2048, 4096], P('dp', 'seq'), may hold values from -512 to 512
- key_rows: bfloat16 [16, 2048, 4096], P('dp', 'seq'), may hold values from -18 to 18
- value_rows: bfloat16 [16, 2048, 4096], P('dp', 'seq'), may hold values from -6 to 6
- w_out: bfloat16 [4096, 3072], P('seq', 'dp'), may hold values from -1.5 to 1.5
Outputs:
- attn_output: bfloat16 [16, 2048, 3072], P('dp', 'seq')
The draws below stay inside these ranges and needn't reach their ends.
All inputs are finite; a program needn't handle non-finite values.
Results may differ from the reference program's by a relative error of at most 0.0095.
Values may be sent and summed in bfloat16 or wider, within the bound.
No kernel may reach another device: no remote copies, remote signals or barrier semaphores. Data moves between devices by JAX's collectives and lax.ppermute only.
A program may use at most 128 MiB of HBM per device.

```python
import jax
import jax.numpy as jnp
from jax import lax

HEADS = 32
HEAD_DIM = 128
DOUT = 3072
LEN = 2048
CLIPS = 16
N_SEQ = 16


def draw_pair(key):
    base = jax.random.fold_in(key, 7)
    key_query, key_keys = jax.random.split(base, 2)
    width = HEADS * HEAD_DIM
    queries = jax.random.truncated_normal(key_query, -6.0, 6.0, (CLIPS, LEN, width), jnp.float32)
    keys_all = jax.random.truncated_normal(key_keys, -6.0, 6.0, (CLIPS, LEN, width), jnp.float32)
    return (queries, keys_all)


def draw_queries(key, part):
    return draw_pair(key)[0].astype(jnp.bfloat16)


def draw_key_rows(key, part):
    return draw_pair(key)[1].astype(jnp.bfloat16)


def level_of(own_key, shape, cuts, smallest, high):
    factor_of = 1.0
    for dim, parts in cuts:
        draws = jax.random.uniform(jax.random.fold_in(jax.random.fold_in(own_key, 6), dim), (parts,), jnp.float32, smallest / len(cuts), high / len(cuts))
        factor_of = factor_of * jnp.repeat(jnp.exp(draws), shape[dim] // parts).reshape((-1,) + (1,) * (len(shape) - 1 - dim))
    return factor_of


def noise(key, extent, scale, reach, shards=(), dtype=jnp.bfloat16):
    level = level_of(key, extent, shards, -0.22, 0.18) if shards else 1.0
    drawn = jax.random.normal(key, extent, jnp.float32) * scale * level
    return jnp.minimum(jnp.maximum(drawn, -reach), reach).astype(dtype)


def setup_inputs(seed: int = 0) -> dict:
    key_of = jax.random.split(jax.random.key(seed), 5)
    return {
        "queries": draw_queries(jax.random.fold_in(key_of[4], 71), 0),
        "key_rows": draw_key_rows(jax.random.fold_in(key_of[4], 71), 0),
        "value_rows": noise(key_of[2], (CLIPS, LEN, HEADS * HEAD_DIM), 1.0, 6.0, ((0, 16), (1, 16))),
        "w_out": noise(key_of[3], (HEADS * HEAD_DIM, DOUT), (max(HEADS * HEAD_DIM // 256, 1)) ** -0.5, 1.5, ((0, 16), (1, 16))),
    }


def attend_block(qblock, keys_all, values_all, factor):
    scores = jnp.einsum("qhd,khd->hqk", qblock, keys_all) * factor
    largest = jnp.max(scores, axis=2, keepdims=True)
    weights = jnp.exp(scores - largest)
    totals = jnp.sum(weights, axis=2, keepdims=True)
    probs = (weights / totals).astype(jnp.bfloat16)
    probs = lax.optimization_barrier(probs).astype(jnp.float32)
    mixed = jnp.einsum("hqk,khd->qhd", probs, values_all)
    return mixed.astype(jnp.bfloat16)


def one_clip(triple, w_out):
    queries, keys_all, values_all = triple
    length = queries.shape[0]
    width = queries.shape[1]
    heads = width // HEAD_DIM
    block = min(512, length)
    factor = HEAD_DIM ** -0.5
    blocked = queries.astype(jnp.float32).reshape(length // block, block, heads, HEAD_DIM)
    keys_all = keys_all.astype(jnp.float32).reshape(length, heads, HEAD_DIM)
    values_all = values_all.astype(jnp.float32).reshape(length, heads, HEAD_DIM)
    outcome = lax.map(lambda qblock: attend_block(qblock, keys_all, values_all, factor), blocked)
    grouped = outcome.astype(jnp.float32).reshape(length, N_SEQ, width // N_SEQ)
    weight_groups = w_out.astype(jnp.float32).reshape(N_SEQ, width // N_SEQ, w_out.shape[1])
    group_part = jnp.einsum("tgk,gkc->gtc", grouped, weight_groups).astype(jnp.bfloat16)
    group_part = lax.optimization_barrier(group_part).astype(jnp.float32)
    return jnp.sum(group_part, axis=0).astype(jnp.bfloat16)


def reference(queries, key_rows, value_rows, w_out):
    return lax.map(lambda triple: one_clip(triple, w_out), (queries, key_rows, value_rows))
```

```python
import functools

import jax
import jax.numpy as jnp
import numpy as np
from jax import lax
from jax.experimental import pallas as pl
from jax.experimental.pallas import tpu as pltpu
from jax.sharding import Mesh
from jax.sharding import PartitionSpec as P

HEAD_DIM = 128
SCALE = float(np.log2(np.e) / np.sqrt(HEAD_DIM))
DP = ("yh", "x", "core")
SEQ = ("yl", "z")
BF16 = jnp.bfloat16
F32 = jnp.float32


def cost(flops, nbytes, exps=0):
    return pl.CostEstimate(flops=flops, bytes_accessed=nbytes, transcendentals=exps)


def pack_kernel(head, q_ref, k_ref, v_ref, out_ref):
    for index, ref in enumerate((q_ref, k_ref, v_ref)):
        for group in range(out_ref.shape[0]):
            low = group * 256 + head * HEAD_DIM
            out_ref[group, index] = ref[:, low : low + HEAD_DIM]


def pack(queries, key_rows, value_rows, head):
    tokens = queries.shape[0]
    spec = pl.BlockSpec((tokens, 1024), lambda i: (0, i))
    return pl.pallas_call(
        functools.partial(pack_kernel, head),
        grid=(4,),
        in_specs=[spec] * 3,
        out_specs=pl.BlockSpec((4, 3, tokens, HEAD_DIM), lambda i: (i, 0, 0, 0)),
        out_shape=jax.ShapeDtypeStruct((16, 3, tokens, HEAD_DIM), BF16),
        cost_estimate=cost(0, 5 << 20),
        name=f"pack{head}",
    )(queries, key_rows, value_rows)


def attend_kernel(sub, q_ref, k_ref, v_ref, o_ref):
    keys = k_ref[:, 0].reshape(-1, HEAD_DIM)
    values = v_ref[:, 0].reshape(-1, HEAD_DIM)
    rows = q_ref[:, 0].reshape(-1, HEAD_DIM)
    pieces = []
    for low in range(0, rows.shape[0], sub):
        scores = lax.dot_general(
            rows[low : low + sub], keys, (((1,), (1,)), ((), ())), preferred_element_type=F32
        )
        largest = jnp.max(scores, axis=1, keepdims=True)
        weights = jnp.exp2((scores - largest) * SCALE)
        total = jnp.sum(weights, axis=1, keepdims=True)
        mixed = jnp.dot(weights.astype(BF16), values, preferred_element_type=F32)
        pieces.append((mixed / total).astype(BF16))
    o_ref[...] = jnp.concatenate(pieces, 0).reshape(o_ref.shape)


def attend(arrived, head):
    n, _, tokens, _ = arrived.shape
    per = 8
    return pl.pallas_call(
        functools.partial(attend_kernel, 256),
        grid=(n // per,),
        in_specs=[
            pl.BlockSpec((per, 1, tokens, HEAD_DIM), lambda i: (i, 0, 0, 0)),
            pl.BlockSpec((n, 1, tokens, HEAD_DIM), lambda i: (0, 1, 0, 0)),
            pl.BlockSpec((n, 1, tokens, HEAD_DIM), lambda i: (0, 2, 0, 0)),
        ],
        out_specs=pl.BlockSpec((per, tokens, HEAD_DIM), lambda i: (i, 0, 0)),
        out_shape=jax.ShapeDtypeStruct((n, tokens, HEAD_DIM), BF16),
        compiler_params=pltpu.CompilerParams(vmem_limit_bytes=48 << 20),
        cost_estimate=cost(4 * 2048 * 2048 * 128, 2 << 20, 2048 * 2048),
        name=f"attend{head}",
    )(arrived, arrived, arrived)


Z_OFFSETS = (0, -1, 1, -2, 2, -3, 3, -4)
X_OFFSETS = (0, -1, 1, 2)


def gather_features(pos_ref, a_ref, b_ref, a_rel):
    tokens = a_ref.shape[1]
    yl, z = pos_ref[1], pos_ref[2]
    for half in range(2):
        group_y = yl if half == 0 else 1 - yl
        for i, offset in enumerate(Z_OFFSETS):
            group = group_y * 8 + lax.rem(z + (8 + offset), 8)
            low = (half * 8 + i) * HEAD_DIM
            a_rel[:tokens, low : low + HEAD_DIM] = a_ref[group]
            a_rel[tokens:, low : low + HEAD_DIM] = b_ref[group]


def rows_dot(first, second, a_rel):
    w = jnp.concatenate([first[i] for i in range(8)] + [second[i] for i in range(8)], axis=1)
    return lax.dot_general(w, a_rel[...], (((1,), (1,)), ((), ())), preferred_element_type=F32)


def project0_kernel(pos_ref, a_ref, b_ref, own, pair, cross, far, acc_ref, a_rel):
    @pl.when(pl.program_id(0) == 0)
    def _():
        gather_features(pos_ref, a_ref, b_ref, a_rel)

    yh = pos_ref[0]
    acc_ref[yh, 0] = rows_dot(own.at[0], pair.at[0], a_rel)
    acc_ref[1 - yh, 0] = rows_dot(far.at[0], cross.at[0], a_rel)


def x_of(j, pos_ref):
    offset = jnp.where(j == 0, 0, jnp.where(j == 1, 3, jnp.where(j == 2, 1, 2)))
    return lax.rem(pos_ref[3] + offset, 4)


def project0(pos, a, b, blocks):
    tokens = a.shape[1]
    feature = pl.BlockSpec(a.shape, lambda j, p: (0, 0, 0))
    weight = pl.BlockSpec((1, 8, 192, HEAD_DIM), lambda j, p: (j, 0, 0, 0))
    return pl.pallas_call(
        project0_kernel,
        grid_spec=pltpu.PrefetchScalarGridSpec(
            num_scalar_prefetch=1,
            grid=(4,),
            in_specs=[feature, feature] + [weight] * 4,
            out_specs=pl.BlockSpec((2, 1, 192, 2 * tokens), lambda j, p: (0, x_of(j, p), 0, 0)),
            scratch_shapes=[pltpu.VMEM((2 * tokens, 16 * HEAD_DIM), BF16)],
        ),
        out_shape=jax.ShapeDtypeStruct((2, 4, 192, 2 * tokens), F32),
        cost_estimate=cost(2 * 256 * 2048 * 1536, 9 << 20),
        name="project0",
    )(pos, a, b, *blocks)


def project1_kernel(pos_ref, a_ref, b_ref, x0, x1, x2, x3, acc_ref, mine_ref, theirs_ref, a_rel):
    step = pl.program_id(0)

    @pl.when(step == 0)
    def _():
        gather_features(pos_ref, a_ref, b_ref, a_rel)

    tokens = mine_ref.shape[3]

    def emit(same):
        for j, block in enumerate((x0, x1, x2, x3)):
            x = lax.rem(pos_ref[3] + (4 + X_OFFSETS[j]), 4)
            pair = (block.at[0], block.at[1]) if same else (block.at[1], block.at[0])
            total = acc_ref[0, x] + rows_dot(*pair, a_rel)
            mine_ref[0, x] = total[:, :tokens].astype(BF16)
            theirs_ref[0, x] = total[:, tokens:].astype(BF16)

    @pl.when(step == 0)
    def _():
        emit(True)

    @pl.when(step == 1)
    def _():
        emit(False)


def project1(pos, a, b, blocks, acc):
    tokens = a.shape[1]
    feature = pl.BlockSpec(a.shape, lambda j, p: (0, 0, 0))
    weight = pl.BlockSpec((2, 8, 192, HEAD_DIM), lambda j, p: (j, 0, 0, 0))

    def row(j, p):
        return (jnp.where(j == 0, p[0], 1 - p[0]), 0, 0, 0)

    shape = jax.ShapeDtypeStruct((2, 4, 192, tokens), BF16)
    return pl.pallas_call(
        project1_kernel,
        grid_spec=pltpu.PrefetchScalarGridSpec(
            num_scalar_prefetch=1,
            grid=(2,),
            in_specs=[feature, feature]
            + [weight] * 4
            + [pl.BlockSpec((1, 4, 192, 2 * tokens), row)],
            out_specs=[pl.BlockSpec((1, 4, 192, tokens), row)] * 2,
            scratch_shapes=[pltpu.VMEM((2 * tokens, 16 * HEAD_DIM), BF16)],
        ),
        out_shape=[shape, shape],
        cost_estimate=cost(2 * 256 * 2048 * 1536, 9 << 20),
        name="project1",
    )(pos, a, b, *blocks, acc)


def finish_kernel(pos_ref, mine_ref, other_ref, out_ref, stack):
    core = pos_ref[4]
    for yh in range(2):
        for x in range(4):
            stack[pl.ds(pl.multiple_of(core * 192, 64), 192)] = mine_ref[yh, x].astype(F32)
            stack[pl.ds(pl.multiple_of((1 - core) * 192, 64), 192)] = other_ref[yh, x].astype(F32)
            low = (yh * 4 + x) * 384
            out_ref[:, low : low + 384] = stack[...].T.astype(BF16)


def finish(pos, mine, other):
    tokens = mine.shape[3]
    whole = pl.BlockSpec(mine.shape, lambda i, p: (0, 0, 0, 0))
    return pl.pallas_call(
        finish_kernel,
        grid_spec=pltpu.PrefetchScalarGridSpec(
            num_scalar_prefetch=1,
            grid=(1,),
            in_specs=[whole, whole],
            out_specs=pl.BlockSpec((tokens, 3072), lambda i, p: (0, 0)),
            scratch_shapes=[pltpu.VMEM((384, tokens), F32)],
        ),
        out_shape=jax.ShapeDtypeStruct((tokens, 3072), BF16),
        cost_estimate=cost(0, 2 << 20),
        name="finish",
    )(pos, mine, other)


def shift(value, axis, size, step):
    return lax.ppermute(value, axis, [(i, (i + step) % size) for i in range(size)])


def pair_swap(value):
    return lax.ppermute(value, "yl", [(0, 1), (1, 0)])


def cross_swap(value):
    return lax.ppermute(value, ("yh", "yl"), [(1, 2), (2, 1), (3, 0), (0, 3)])


def core_swap(value):
    return lax.ppermute(value, "core", [(0, 1), (1, 0)])


def z_blocks(wt):
    up1, down1 = shift(wt, "z", 8, 1), shift(wt, "z", 8, -1)
    up2, down2 = shift(up1, "z", 8, 1), shift(down1, "z", 8, -1)
    up3, down3 = shift(up2, "z", 8, 1), shift(down2, "z", 8, -1)
    up4 = shift(up3, "z", 8, 1)
    return [wt, up1, down1, up2, down2, up3, down3, up4]


def x_blocks(block):
    return [block, shift(block, "x", 4, 1), shift(block, "x", 4, -1), shift(block, "x", 4, 2)]


def y_blocks(block):
    pair, cross = pair_swap(block), cross_swap(block)
    return [block, pair, cross, cross_swap(pair)]


def all_to_all(value):
    return lax.all_to_all(value, SEQ, 0, 0, tiled=True)


def per_device(queries, key_rows, value_rows, w_out):
    q, k, v = queries[0], key_rows[0], value_rows[0]
    pos = jnp.stack([lax.axis_index(n) for n in ("yh", "yl", "z", "x", "core")]).astype(jnp.int32)

    sent0 = all_to_all(pack(q, k, v, 0))
    blocks = z_blocks(w_out.T)
    half0 = jnp.stack([block[:, :HEAD_DIM] for block in blocks])
    half1 = jnp.stack([block[:, HEAD_DIM:] for block in blocks])
    weights0 = y_blocks(jnp.stack(x_blocks(half0)))
    weights1 = x_blocks(jnp.stack(y_blocks(half1)))

    sent1 = all_to_all(pack(q, k, v, 1))
    back0 = all_to_all(attend(sent0, 0))
    back1 = all_to_all(attend(sent1, 1))
    acc = project0(pos, back0, core_swap(back0), weights0)
    mine, theirs = project1(pos, back1, core_swap(back1), weights1, acc)
    return finish(pos, mine, core_swap(theirs))[None]


def solution(mesh):
    fine = Mesh(mesh.devices.reshape(2, 4, 2, 2, 8), DP + SEQ)
    rows = P(DP, SEQ, None)
    return jax.shard_map(
        per_device,
        mesh=fine,
        in_specs=(rows, rows, rows, P(SEQ, DP)),
        out_specs=rows,
        check_vma=False,
    )
```

```python
import functools

import jax
import jax.numpy as jnp
import numpy as np
from jax import lax
from jax.experimental import pallas as pl
from jax.experimental.pallas import tpu as pltpu
from jax.sharding import Mesh
from jax.sharding import PartitionSpec as P

HEAD_DIM = 128
SCALE = float(np.log2(np.e) / np.sqrt(HEAD_DIM))
DP = ("yh", "x", "core")
SEQ = ("yl", "z")
BF16 = jnp.bfloat16
F32 = jnp.float32


def cost(flops, nbytes, exps=0):
    return pl.CostEstimate(flops=flops, bytes_accessed=nbytes, transcendentals=exps)


def pack_kernel(head, q_ref, k_ref, v_ref, out_ref):
    for index, ref in enumerate((q_ref, k_ref, v_ref)):
        for group in range(out_ref.shape[0]):
            low = group * 256 + head * HEAD_DIM
            out_ref[group, index] = ref[:, low : low + HEAD_DIM]


def pack(queries, key_rows, value_rows, head):
    tokens = queries.shape[0]
    spec = pl.BlockSpec((tokens, 1024), lambda i: (0, i))
    return pl.pallas_call(
        functools.partial(pack_kernel, head),
        grid=(4,),
        in_specs=[spec] * 3,
        out_specs=pl.BlockSpec((4, 3, tokens, HEAD_DIM), lambda i: (i, 0, 0, 0)),
        out_shape=jax.ShapeDtypeStruct((16, 3, tokens, HEAD_DIM), BF16),
        cost_estimate=cost(0, 5 << 20),
    )(queries, key_rows, value_rows)


def attend_kernel(sub, q_ref, k_ref, v_ref, o_ref):
    keys = k_ref[:, 0].reshape(-1, HEAD_DIM)
    values = v_ref[:, 0].reshape(-1, HEAD_DIM)
    rows = q_ref[:, 0].reshape(-1, HEAD_DIM)
    pieces = []
    for low in range(0, rows.shape[0], sub):
        scores = lax.dot_general(
            rows[low : low + sub], keys, (((1,), (1,)), ((), ())), preferred_element_type=F32
        )
        largest = jnp.max(scores, axis=1, keepdims=True)
        weights = jnp.exp2((scores - largest) * SCALE)
        total = jnp.sum(weights, axis=1, keepdims=True)
        mixed = jnp.dot(weights.astype(BF16), values, preferred_element_type=F32)
        pieces.append((mixed / total).astype(BF16))
    o_ref[...] = jnp.concatenate(pieces, 0).reshape(o_ref.shape)


def attend(arrived):
    n, _, tokens, _ = arrived.shape
    per = 4
    return pl.pallas_call(
        functools.partial(attend_kernel, 256),
        grid=(n // per,),
        in_specs=[
            pl.BlockSpec((per, 1, tokens, HEAD_DIM), lambda i: (i, 0, 0, 0)),
            pl.BlockSpec((n, 1, tokens, HEAD_DIM), lambda i: (0, 1, 0, 0)),
            pl.BlockSpec((n, 1, tokens, HEAD_DIM), lambda i: (0, 2, 0, 0)),
        ],
        out_specs=pl.BlockSpec((per, tokens, HEAD_DIM), lambda i: (i, 0, 0)),
        out_shape=jax.ShapeDtypeStruct((n, tokens, HEAD_DIM), BF16),
        compiler_params=pltpu.CompilerParams(vmem_limit_bytes=48 << 20),
        cost_estimate=cost(4 * 2048 * 2048 * 128, 2 << 20, 2048 * 2048),
    )(arrived, arrived, arrived)


NEAR = (0, -1, 1, -2, 2)
FAR = (-3, 3, -4)
Z_OFFSETS = NEAR + FAR
X_OFFSETS = (0, -1, 1, 2)
ROWS_A, ROWS_B = 80, 112


def gather_features(pos_ref, a_ref, b_ref, a_rel):
    tokens = a_ref.shape[1]
    yl, z = pos_ref[1], pos_ref[2]
    for half in range(2):
        group_y = yl if half == 0 else 1 - yl
        for i, offset in enumerate(Z_OFFSETS):
            group = group_y * 8 + lax.rem(z + (8 + offset), 8)
            low = (half * 8 + i) * HEAD_DIM
            a_rel[:tokens, low : low + HEAD_DIM] = a_ref[group]
            a_rel[tokens:, low : low + HEAD_DIM] = b_ref[group]


def weight_rows(groups, same):
    columns = []
    for half in range(2):
        for own, pair, cross, far, x0, x1, x2, x3a, x3b in groups:
            part_a = ((own, pair) if same else (far, cross))[half]
            y = ((0, 1) if same else (3, 2))[half]
            part_x3 = (x3a, x3b)[y // 2]
            for i in range(own.shape[1]):
                rows = [part_a[:, i].reshape(4 * ROWS_A, HEAD_DIM)]
                rows += [x0[y, i], x1[y, i], x2[y, i], part_x3[y % 2, i]]
                columns.append(jnp.concatenate(rows, axis=0))
    return jnp.concatenate(columns, axis=1)


def project_kernel(head, pos_ref, a_ref, b_ref, *refs):
    groups = (refs[:9], refs[9:18])
    a_rel = refs[-1]
    gather_features(pos_ref, a_ref, b_ref, a_rel)
    tokens = a_ref.shape[1]
    for same in (True, False):
        yh = pos_ref[0] if same else 1 - pos_ref[0]
        total = lax.dot_general(
            weight_rows(groups, same),
            a_rel[...],
            (((1,), (1,)), ((), ())),
            preferred_element_type=F32,
        )
        for j, offset in enumerate(X_OFFSETS):
            x = lax.rem(pos_ref[3] + (4 + offset), 4)
            first = 4 * ROWS_A + j * ROWS_B
            parts = (
                (0, ROWS_A, total[j * ROWS_A : (j + 1) * ROWS_A]),
                (ROWS_A, 192, total[first : first + ROWS_B]),
            )
            for low, high, part in parts:
                if head == 0:
                    refs[18][yh, x, low:high] = part
                else:
                    part = part + refs[18][yh, x, low:high]
                    refs[19][yh, x, low:high] = part[:, :tokens].astype(BF16)
                    refs[20][yh, x, low:high] = part[:, tokens:].astype(BF16)


def project(pos, a, b, groups, head, acc=None):
    tokens = a.shape[1]
    whole = pl.BlockSpec(memory_space=pltpu.VMEM)
    buffers = [buffer for group in groups for buffer in group]

    def half(buffer):
        return pl.BlockSpec((*buffer.shape[:3], HEAD_DIM), lambda i, p: (0, 0, 0, head))

    if head == 0:
        shapes = jax.ShapeDtypeStruct((2, 4, 192, 2 * tokens), F32)
        out_specs, extra = whole, []
    else:
        shapes = [jax.ShapeDtypeStruct((2, 4, 192, tokens), BF16)] * 2
        out_specs, extra = [whole, whole], [acc]
    return pl.pallas_call(
        functools.partial(project_kernel, head),
        grid_spec=pltpu.PrefetchScalarGridSpec(
            num_scalar_prefetch=1,
            grid=(1,),
            in_specs=[whole, whole] + [half(buffer) for buffer in buffers] + [whole] * len(extra),
            out_specs=out_specs,
            scratch_shapes=[pltpu.VMEM((2 * tokens, 16 * HEAD_DIM), BF16)],
        ),
        out_shape=shapes,
        compiler_params=pltpu.CompilerParams(vmem_limit_bytes=48 << 20),
        cost_estimate=cost(2 * 256 * 2048 * 1536, 9 << 20),
    )(pos, a, b, *buffers, *extra)


def finish_kernel(pos_ref, mine_ref, other_ref, out_ref, stack):
    core = pos_ref[4]
    for yh in range(2):
        for x in range(4):
            stack[pl.ds(pl.multiple_of(core * 192, 64), 192)] = mine_ref[yh, x].astype(F32)
            stack[pl.ds(pl.multiple_of((1 - core) * 192, 64), 192)] = other_ref[yh, x].astype(F32)
            low = (yh * 4 + x) * 384
            out_ref[:, low : low + 384] = stack[...].T.astype(BF16)


def finish(pos, mine, other):
    tokens = mine.shape[3]
    whole = pl.BlockSpec(mine.shape, lambda i, p: (0, 0, 0, 0))
    return pl.pallas_call(
        finish_kernel,
        grid_spec=pltpu.PrefetchScalarGridSpec(
            num_scalar_prefetch=1,
            grid=(1,),
            in_specs=[whole, whole],
            out_specs=pl.BlockSpec((tokens, 3072), lambda i, p: (0, 0)),
            scratch_shapes=[pltpu.VMEM((384, tokens), F32)],
        ),
        out_shape=jax.ShapeDtypeStruct((tokens, 3072), BF16),
        cost_estimate=cost(0, 2 << 20),
        name="finish",
    )(pos, mine, other)


def shift(value, axis, size, step):
    return lax.ppermute(value, axis, [(i, (i + step) % size) for i in range(size)])


def pair_swap(value):
    return lax.ppermute(value, "yl", [(0, 1), (1, 0)])


def cross_swap(value):
    return lax.ppermute(value, ("yh", "yl"), [(1, 2), (2, 1), (3, 0), (0, 3)])


def core_swap(value):
    return lax.ppermute(value, "core", [(0, 1), (1, 0)])


def split_kernel(*refs):
    *blocks, a_ref, b_ref = refs
    for i, block in enumerate(blocks):
        a_ref[i] = block[:ROWS_A]
        b_ref[i] = block[ROWS_A:]


def split_rows(blocks):
    depth = blocks[0].shape[1]
    return pl.pallas_call(
        split_kernel,
        out_shape=[
            jax.ShapeDtypeStruct((len(blocks), rows, depth), BF16) for rows in (ROWS_A, ROWS_B)
        ],
        cost_estimate=cost(0, 1 << 20),
    )(*blocks)


def spread(blocks):
    a, b = split_rows(blocks)
    ax = [a, shift(a, "x", 4, 1), shift(a, "x", 4, -1), shift(a, "x", 4, 2)]
    b_pair, b_cross = pair_swap(b), cross_swap(b)
    by = [b, b_pair, b_cross, cross_swap(b_pair)]
    a, b = jnp.stack(ax), jnp.stack(by)
    a_pair, a_cross = pair_swap(a), cross_swap(a)
    b_up, b_down = shift(b, "x", 4, 1), shift(b, "x", 4, -1)
    a_far = cross_swap(a_pair)
    b_far = (shift(b_up[:2], "x", 4, 1), shift(b_down[2:], "x", 4, -1))
    return (a, a_pair, a_cross, a_far, b, b_up, b_down, *b_far)


def all_to_all(value):
    return lax.all_to_all(value, SEQ, 0, 0, tiled=True)


def per_device(queries, key_rows, value_rows, w_out):
    q, k, v = queries[0], key_rows[0], value_rows[0]
    pos = jnp.stack([lax.axis_index(n) for n in ("yh", "yl", "z", "x", "core")]).astype(jnp.int32)
    wt = w_out.T

    near = {step: shift(wt, "z", 8, -step) for step in NEAR[1:]}
    sent0 = all_to_all(pack(q, k, v, 0))
    far = {
        -3: shift(near[-2], "z", 8, 1),
        3: shift(near[2], "z", 8, -1),
        -4: shift(near[-2], "z", 8, 2),
    }
    weights0 = spread([wt] + [near[step] for step in NEAR[1:]])
    weights1 = spread([far[step] for step in FAR])

    sent1 = all_to_all(pack(q, k, v, 1))
    mixed0 = attend(sent0)
    back0 = all_to_all(mixed0)
    mixed1 = attend(sent1)
    back1 = all_to_all(mixed1)
    groups = (weights0, weights1)
    other0 = core_swap(back0)
    acc = project(pos, back0, other0, groups, 0)
    mine, theirs = project(pos, back1, core_swap(back1), groups, 1, acc)
    return finish(pos, mine, core_swap(theirs))[None]


def solution(mesh):
    fine = Mesh(mesh.devices.reshape(2, 4, 2, 2, 8), DP + SEQ)
    rows = P(DP, SEQ, None)
    return jax.shard_map(
        per_device,
        mesh=fine,
        in_specs=(rows, rows, rows, P(SEQ, DP)),
        out_specs=rows,
        check_vma=False,
    )
```

```python
import functools

import jax
import jax.numpy as jnp
import numpy as np
from jax import lax
from jax.experimental import pallas as pl
from jax.experimental.pallas import tpu as pltpu
from jax.sharding import Mesh
from jax.sharding import PartitionSpec as P

HEAD_DIM = 128
SCALE = float(np.log2(np.e) / np.sqrt(HEAD_DIM))
DP = ("yh", "x", "core")
SEQ = ("yl", "z")
BF16 = jnp.bfloat16
F32 = jnp.float32


def cost(flops, nbytes, exps=0):
    return pl.CostEstimate(flops=flops, bytes_accessed=nbytes, transcendentals=exps)


def pack_kernel(head, q_ref, k_ref, v_ref, out_ref, sem):
    copies = [
        pltpu.make_async_copy(
            ref.at[:, pl.ds(group * 256 + head * HEAD_DIM, HEAD_DIM)],
            out_ref.at[group, index],
            sem.at[group, index],
        )
        for group in range(16)
        for index, ref in enumerate((q_ref, k_ref, v_ref))
    ]
    for copy in copies:
        copy.start()
    for copy in copies:
        copy.wait()


def pack(queries, key_rows, value_rows, head):
    tokens = queries.shape[0]
    return pl.pallas_call(
        functools.partial(pack_kernel, head),
        in_specs=[pl.BlockSpec(memory_space=pltpu.HBM)] * 3,
        out_shape=pltpu.HBM((16, 3, tokens, HEAD_DIM), BF16),
        scratch_shapes=[pltpu.SemaphoreType.DMA((16, 3))],
        compiler_params=pltpu.CompilerParams(vmem_limit_bytes=60 * 1024 * 1024),
        cost_estimate=cost(0, 5 << 20),
    )(queries, key_rows, value_rows)


def attend_rows(rows, keys, values):
    scores = lax.dot_general(
        rows, keys, (((1,), (1,)), ((), ())), preferred_element_type=F32
    )
    largest = jnp.max(scores, axis=1, keepdims=True)
    weights = jnp.exp2((scores - largest) * SCALE)
    total = jnp.sum(weights, axis=1, keepdims=True)
    mixed = jnp.dot(weights.astype(BF16), values, preferred_element_type=F32)
    return (mixed / total).astype(BF16)


def attend_kernel(sub, q_ref, k_ref, v_ref, o_ref):
    keys = k_ref[:, 0].reshape(-1, HEAD_DIM)
    values = v_ref[:, 0].reshape(-1, HEAD_DIM)
    rows = q_ref[:, 0].reshape(-1, HEAD_DIM)
    pieces = [
        attend_rows(rows[low : low + sub], keys, values) for low in range(0, rows.shape[0], sub)
    ]
    o_ref[...] = jnp.concatenate(pieces, 0).reshape(o_ref.shape)


def attend(arrived):
    n, _, tokens, _ = arrived.shape
    per = 4
    return pl.pallas_call(
        functools.partial(attend_kernel, 256),
        grid=(n // per,),
        in_specs=[
            pl.BlockSpec((per, 1, tokens, HEAD_DIM), lambda i: (i, 0, 0, 0)),
            pl.BlockSpec((n, 1, tokens, HEAD_DIM), lambda i: (0, 1, 0, 0)),
            pl.BlockSpec((n, 1, tokens, HEAD_DIM), lambda i: (0, 2, 0, 0)),
        ],
        out_specs=pl.BlockSpec((per, tokens, HEAD_DIM), lambda i: (i, 0, 0)),
        out_shape=pltpu.HBM((n, tokens, HEAD_DIM), BF16),
        compiler_params=pltpu.CompilerParams(vmem_limit_bytes=24 << 20),
        cost_estimate=cost(4 * 2048 * 2048 * 128, 2 << 20, 2048 * 2048),
    )(arrived, arrived, arrived)


NEAR = (0, -1, 1, -2, 2)
FAR = (-3, 3, -4)
Z_OFFSETS = NEAR + FAR
X_OFFSETS = (0, -1, 1, 2)
ROWS_A, ROWS_B = 80, 112


def gather_features(pos_ref, features, a_rel):
    tokens = features.shape[2]
    yl, z = pos_ref[1], pos_ref[2]
    for half in range(2):
        group_y = yl if half == 0 else 1 - yl
        for i, offset in enumerate(Z_OFFSETS):
            group = group_y * 8 + lax.rem(z + (8 + offset), 8)
            low = (half * 8 + i) * HEAD_DIM
            for core in range(2):
                a_rel[core * tokens : (core + 1) * tokens, low : low + HEAD_DIM] = features[
                    core, group
                ]


def weight_rows(buffers, same):
    own, pair, cross, far, *b_parts = buffers
    columns = []
    for half in range(2):
        part_a = ((own, pair) if same else (far, cross))[half]
        y = ((0, 1) if same else (3, 2))[half]
        for i in range(own.shape[1]):
            rows = [part_a[:, i].reshape(4 * ROWS_A, HEAD_DIM)]
            rows += [b_parts[2 * j + y // 2][y % 2, i] for j in range(4)]
            columns.append(jnp.concatenate(rows, axis=0))
    return jnp.concatenate(columns, axis=1)


def load_kernel(head, *refs):
    count = len(refs[1:-1]) // 2
    sources, targets, sem = refs[1 : 1 + count], refs[1 + count : -1], refs[-1]
    copies = [
        pltpu.make_async_copy(source.at[:, :, head], target, sem.at[i])
        for i, (source, target) in enumerate(zip(sources, targets))
    ]
    for copy in copies:
        copy.start()
    for copy in copies:
        copy.wait()


def load(ready, buffers, head):
    shapes = [(*buffer.shape[:2], *buffer.shape[3:]) for buffer in buffers]
    return pl.pallas_call(
        functools.partial(load_kernel, head),
        in_specs=[pl.BlockSpec(memory_space=pl.ANY)] * (1 + len(buffers)),
        out_specs=[pl.BlockSpec(memory_space=pltpu.VMEM)] * len(buffers),
        out_shape=[jax.ShapeDtypeStruct(shape, BF16) for shape in shapes],
        scratch_shapes=[pltpu.SemaphoreType.DMA((len(buffers),))],
        compiler_params=pltpu.CompilerParams(vmem_limit_bytes=16 << 20),
        cost_estimate=cost(0, 8 << 20),
    )(ready, *buffers)


def project_kernel(head, pos_ref, a_ref, b_ref, *refs):
    buffers, refs = refs[:12], refs[12:]
    if head == 0:
        out_ref, features, a_rel, sem = refs
    else:
        acc_ref, mine_ref, theirs_ref, features, a_rel, sem = refs
    copies = [
        pltpu.make_async_copy(ref, features.at[i], sem.at[i])
        for i, ref in enumerate((a_ref, b_ref))
    ]
    for copy in copies:
        copy.start()
    for copy in copies:
        copy.wait()
    gather_features(pos_ref, features, a_rel)
    tokens = a_ref.shape[1]
    for same in (True, False):
        yh = pos_ref[0] if same else 1 - pos_ref[0]
        total = lax.dot_general(
            weight_rows(buffers, same),
            a_rel[...],
            (((1,), (1,)), ((), ())),
            preferred_element_type=F32,
        )
        for j, offset in enumerate(X_OFFSETS):
            x = lax.rem(pos_ref[3] + (4 + offset), 4)
            first = 4 * ROWS_A + j * ROWS_B
            parts = (
                (0, ROWS_A, total[j * ROWS_A : (j + 1) * ROWS_A]),
                (ROWS_A, 192, total[first : first + ROWS_B]),
            )
            for low, high, part in parts:
                if head == 0:
                    out_ref[yh, x, low:high] = part
                else:
                    part = part + acc_ref[yh, x, low:high]
                    mine_ref[yh, x, low:high] = part[:, :tokens].astype(BF16)
                    theirs_ref[yh, x, low:high] = part[:, tokens:].astype(BF16)


def project(pos, a, b, buffers, head, acc=()):
    tokens = a.shape[1]
    anywhere, vmem = (pl.BlockSpec(memory_space=space) for space in (pl.ANY, pltpu.VMEM))
    if head == 0:
        shapes, out_specs = pltpu.HBM((2, 4, 192, 2 * tokens), F32), vmem
    else:
        shapes = [jax.ShapeDtypeStruct((2, 4, 192, tokens), BF16)] * 2
        out_specs = [vmem, vmem]
    return pl.pallas_call(
        functools.partial(project_kernel, head),
        grid_spec=pltpu.PrefetchScalarGridSpec(
            num_scalar_prefetch=1,
            grid=(1,),
            in_specs=[anywhere] * 2 + [vmem] * (len(buffers) + len(acc)),
            out_specs=out_specs,
            scratch_shapes=[
                pltpu.VMEM((2, *a.shape), BF16),
                pltpu.VMEM((2 * tokens, 16 * HEAD_DIM), BF16),
                pltpu.SemaphoreType.DMA((2,)),
            ],
        ),
        out_shape=shapes,
        compiler_params=pltpu.CompilerParams(vmem_limit_bytes=24 << 20),
        cost_estimate=cost(2 * 256 * 2048 * 1536, 9 << 20),
    )(pos, a, b, *buffers, *acc)


def finish_kernel(pos_ref, mine_ref, other_ref, out_ref, mine, other, stack, sem):
    core = pos_ref[4]
    copies = [
        pltpu.make_async_copy(source, target, sem.at[i])
        for i, (source, target) in enumerate(((mine_ref, mine), (other_ref, other)))
    ]
    for copy in copies:
        copy.start()
    for copy in copies:
        copy.wait()
    for yh in range(2):
        for x in range(4):
            block = stack.at[yh * 4 + x]
            block[pl.ds(pl.multiple_of(core * 192, 64), 192)] = mine[yh, x]
            block[pl.ds(pl.multiple_of((1 - core) * 192, 64), 192)] = other[yh, x]
            low = (yh * 4 + x) * 384
            out_ref[:, low : low + 384] = block[...].T


def finish(pos, mine, other):
    tokens = mine.shape[3]
    anywhere = pl.BlockSpec(memory_space=pl.ANY)
    return pl.pallas_call(
        finish_kernel,
        grid_spec=pltpu.PrefetchScalarGridSpec(
            num_scalar_prefetch=1,
            grid=(1,),
            in_specs=[anywhere, anywhere],
            out_specs=pl.BlockSpec((tokens, 3072), lambda i, p: (0, 0)),
            scratch_shapes=[
                pltpu.VMEM(mine.shape, BF16),
                pltpu.VMEM(mine.shape, BF16),
                pltpu.VMEM((8, 384, tokens), BF16),
                pltpu.SemaphoreType.DMA((2,)),
            ],
        ),
        out_shape=jax.ShapeDtypeStruct((tokens, 3072), BF16),
        compiler_params=pltpu.CompilerParams(vmem_limit_bytes=8 << 20),
        cost_estimate=cost(0, 2 << 20),
        name="finish",
    )(pos, mine, other)


def shift(value, axis, size, step):
    return lax.ppermute(value, axis, [(i, (i + step) % size) for i in range(size)])


def pair_swap(value):
    return lax.ppermute(value, "yl", [(0, 1), (1, 0)])


def cross_swap(value):
    return lax.ppermute(value, ("yh", "yl"), [(1, 2), (2, 1), (3, 0), (0, 3)])


def core_swap(value):
    return lax.ppermute(value, "core", [(0, 1), (1, 0)])


def split_kernel(*refs):
    *blocks, a_ref, b_ref = refs
    for i, block in enumerate(blocks):
        for head in range(2):
            lanes = slice(head * HEAD_DIM, (head + 1) * HEAD_DIM)
            a_ref[i, head] = block[:ROWS_A, lanes]
            b_ref[i, head] = block[ROWS_A:, lanes]


def split_rows(blocks):
    return pl.pallas_call(
        split_kernel,
        out_shape=[
            jax.ShapeDtypeStruct((len(blocks), 2, rows, HEAD_DIM), BF16) for rows in (ROWS_A, ROWS_B)
        ],
        compiler_params=pltpu.CompilerParams(vmem_limit_bytes=8 << 20),
        cost_estimate=cost(0, 1 << 20),
    )(*blocks)


def spread(blocks):
    a, b = split_rows(blocks)
    b_pair, b_cross = pair_swap(b), cross_swap(b)
    a_up, a_down = shift(a, "x", 4, 1), shift(a, "x", 4, -1)
    b_far, a_up2 = cross_swap(b_pair), shift(a_up, "x", 4, 1)
    near = jnp.stack([b, b_pair])
    a, far = jnp.stack([a, a_up, a_down, a_up2]), jnp.stack([b_cross, b_far])
    up, down = [shift(near, "x", 4, 1)], [shift(near, "x", 4, -1)]
    a_pair, a_cross = pair_swap(a), cross_swap(a)
    up.append(shift(far, "x", 4, 1))
    down.append(shift(far, "x", 4, -1))
    a_far = cross_swap(a_pair)
    last = [shift(up[0], "x", 4, 1), shift(down[1], "x", 4, -1)]
    return (a, a_pair, a_cross, a_far, near, far, *up, *down, *last)


def all_to_all(value):
    return lax.all_to_all(value, SEQ, 0, 0, tiled=True)


def per_device(queries, key_rows, value_rows, w_out):
    q, k, v = queries[0], key_rows[0], value_rows[0]
    pos = jnp.stack([lax.axis_index(n) for n in ("yh", "yl", "z", "x", "core")]).astype(jnp.int32)
    wt = w_out.T

    near = {step: shift(wt, "z", 8, -step) for step in NEAR[1:]}
    packed0 = pack(q, k, v, 0)
    sent0 = all_to_all(packed0)
    far = {
        -3: shift(near[-2], "z", 8, 1),
        3: shift(near[2], "z", 8, -1),
        -4: shift(near[-2], "z", 8, 2),
    }
    weights = spread([wt] + [near[step] for step in NEAR[1:]] + [far[step] for step in FAR])

    packed1 = pack(q, k, v, 1)
    sent1 = all_to_all(packed1)
    mixed0 = attend(sent0)
    back0 = all_to_all(mixed0)
    mixed1 = attend(sent1)
    back1 = all_to_all(mixed1)
    other0 = core_swap(back0)
    rows0 = load(back0, weights, 0)
    acc = project(pos, back0, other0, rows0, 0)
    other1 = core_swap(back1)
    rows1 = load(back1, weights, 1)
    mine, theirs = project(pos, back1, other1, rows1, 1, (acc,))
    return finish(pos, mine, core_swap(theirs))[None]


def solution(mesh):
    fine = Mesh(mesh.devices.reshape(2, 4, 2, 2, 8), DP + SEQ)
    rows = P(DP, SEQ, None)
    return jax.shard_map(
        per_device,
        mesh=fine,
        in_specs=(rows, rows, rows, P(SEQ, DP)),
        out_specs=rows,
        check_vma=False,
    )
```

```python
import functools

import jax
import jax.numpy as jnp
import numpy as np
from jax import lax
from jax.experimental import pallas as pl
from jax.experimental.pallas import tpu as pltpu
from jax.sharding import Mesh
from jax.sharding import PartitionSpec as P

HEAD_DIM = 128
SCALE = float(np.log2(np.e) / np.sqrt(HEAD_DIM))
DP = ("yh", "x", "core")
SEQ = ("yl", "z")
BF16 = jnp.bfloat16
F32 = jnp.float32


def cost(flops, nbytes, exps=0):
    return pl.CostEstimate(flops=flops, bytes_accessed=nbytes, transcendentals=exps)


def pack_kernel(head, q_ref, k_ref, v_ref, out_ref, stage, in_sem, out_sem):
    loads = [
        [
            pltpu.make_async_copy(
                ref.at[:, pl.ds(group * 256 + head * HEAD_DIM, HEAD_DIM)],
                stage.at[group, index],
                in_sem.at[group, index],
            )
            for index, ref in enumerate((q_ref, k_ref, v_ref))
        ]
        for group in range(16)
    ]
    stores = [
        pltpu.make_async_copy(stage.at[group], out_ref.at[group], out_sem.at[group])
        for group in range(16)
    ]
    for group in loads:
        for copy in group:
            copy.start()
    for group, store in zip(loads, stores):
        for copy in group:
            copy.wait()
        store.start()
    for store in stores:
        store.wait()


def pack(queries, key_rows, value_rows, head):
    shape = (16, 3, queries.shape[0], HEAD_DIM)
    return pl.pallas_call(
        functools.partial(pack_kernel, head),
        in_specs=[pl.BlockSpec(memory_space=pltpu.HBM)] * 3,
        out_specs=pl.BlockSpec(memory_space=pltpu.HBM),
        out_shape=pltpu.HBM(shape, BF16),
        scratch_shapes=[
            pltpu.VMEM(shape, BF16),
            pltpu.SemaphoreType.DMA((16, 3)),
            pltpu.SemaphoreType.DMA((16,)),
        ],
        compiler_params=pltpu.CompilerParams(vmem_limit_bytes=60 * 1024 * 1024),
        cost_estimate=cost(0, 5 << 20),
    )(queries, key_rows, value_rows)


def attend_kernel(sub, q_ref, k_ref, v_ref, o_ref):
    keys = k_ref[:, 0].reshape(-1, HEAD_DIM)
    values = v_ref[:, 0].reshape(-1, HEAD_DIM)
    values = jnp.concatenate([values, jnp.ones_like(values)], axis=1)
    rows = q_ref[:, 0].reshape(-1, HEAD_DIM)
    pieces = []
    for low in range(0, rows.shape[0], sub):
        scores = lax.dot_general(
            rows[low : low + sub], keys, (((1,), (1,)), ((), ())), preferred_element_type=F32
        )
        largest = jnp.max(scores, axis=1, keepdims=True)
        weights = jnp.exp2((scores - largest) * SCALE).astype(BF16)
        mixed = jnp.dot(weights, values, preferred_element_type=F32)
        pieces.append((mixed[:, :HEAD_DIM] / mixed[:, HEAD_DIM:]).astype(BF16))
    o_ref[...] = jnp.concatenate(pieces, 0).reshape(o_ref.shape)


def attend(arrived):
    n, _, tokens, _ = arrived.shape

    def part(index):
        return pl.BlockSpec((n, 1, tokens, HEAD_DIM), lambda i: (0, index, 0, 0))

    return pl.pallas_call(
        functools.partial(attend_kernel, 256),
        grid=(1,),
        in_specs=[part(0), part(1), part(2)],
        out_specs=pl.BlockSpec((n, tokens, HEAD_DIM), lambda i: (0, 0, 0)),
        out_shape=pltpu.HBM((n, tokens, HEAD_DIM), BF16),
        compiler_params=pltpu.CompilerParams(vmem_limit_bytes=40 << 20),
        cost_estimate=cost(4 * 2048 * 2048 * 128, 2 << 20, 2048 * 2048),
    )(arrived, arrived, arrived)


NEAR = (0, -1, 1, -2, 2)
FAR = (-3, 3, -4)
Z_OFFSETS = NEAR + FAR
X_OFFSETS = (0, -1, 1, 2)
ROWS_A, ROWS_B = 64, 128


def gather_features(pos_ref, features, a_rel):
    tokens = features.shape[2]
    yl, z = pos_ref[1], pos_ref[2]
    for half in range(2):
        group_y = yl if half == 0 else 1 - yl
        for i, offset in enumerate(Z_OFFSETS):
            group = group_y * 8 + lax.rem(z + (8 + offset), 8)
            low = (half * 8 + i) * HEAD_DIM
            for core in range(2):
                a_rel[core * tokens : (core + 1) * tokens, low : low + HEAD_DIM] = features[
                    core, group
                ]


def weight_rows(buffers, same):
    own, pair, cross, far, *b_parts = buffers
    columns = []
    for half in range(2):
        part_a = ((own, pair) if same else (far, cross))[half]
        y = ((0, 1) if same else (3, 2))[half]
        for i in range(own.shape[1]):
            rows = [part_a[:, i].reshape(4 * ROWS_A, HEAD_DIM)]
            rows += [b_parts[2 * j + y // 2][y % 2, i] for j in range(4)]
            columns.append(jnp.concatenate(rows, axis=0))
    return jnp.concatenate(columns, axis=1)


def load_kernel(head, *refs):
    count = len(refs[1:-1]) // 2
    sources, targets, sem = refs[1 : 1 + count], refs[1 + count : -1], refs[-1]
    copies = [
        pltpu.make_async_copy(source.at[:, :, head], target, sem.at[i])
        for i, (source, target) in enumerate(zip(sources, targets))
    ]
    for copy in copies:
        copy.start()
    for copy in copies:
        copy.wait()


def load(ready, buffers, head):
    shapes = [(*buffer.shape[:2], *buffer.shape[3:]) for buffer in buffers]
    return pl.pallas_call(
        functools.partial(load_kernel, head),
        in_specs=[pl.BlockSpec(memory_space=pl.ANY)] * (1 + len(buffers)),
        out_specs=[pl.BlockSpec(memory_space=pltpu.VMEM)] * len(buffers),
        out_shape=[jax.ShapeDtypeStruct(shape, BF16) for shape in shapes],
        scratch_shapes=[pltpu.SemaphoreType.DMA((len(buffers),))],
        compiler_params=pltpu.CompilerParams(vmem_limit_bytes=16 << 20),
        cost_estimate=cost(0, 8 << 20),
    )(ready, *buffers)


def project_kernel(head, pos_ref, a_ref, b_ref, *refs):
    buffers, refs = refs[:12], refs[12:]
    if head == 0:
        out_ref, features, a_rel, sem = refs
    else:
        acc_ref, mine_ref, theirs_ref, features, a_rel, sem = refs
    copies = [
        pltpu.make_async_copy(ref, features.at[i], sem.at[i])
        for i, ref in enumerate((a_ref, b_ref))
    ]
    for copy in copies:
        copy.start()
    for copy in copies:
        copy.wait()
    gather_features(pos_ref, features, a_rel)
    tokens = a_ref.shape[1]
    for same in (True, False):
        yh = pos_ref[0] if same else 1 - pos_ref[0]
        total = lax.dot_general(
            weight_rows(buffers, same),
            a_rel[...],
            (((1,), (1,)), ((), ())),
            preferred_element_type=F32,
        )
        for j, offset in enumerate(X_OFFSETS):
            x = lax.rem(pos_ref[3] + (4 + offset), 4)
            first = 4 * ROWS_A + j * ROWS_B
            parts = (
                (0, ROWS_A, total[j * ROWS_A : (j + 1) * ROWS_A]),
                (ROWS_A, 192, total[first : first + ROWS_B]),
            )
            for low, high, part in parts:
                if head == 0:
                    out_ref[yh, x, low:high] = part
                else:
                    part = part + acc_ref[yh, x, low:high]
                    mine_ref[yh, x, low:high] = part[:, :tokens].astype(BF16)
                    theirs_ref[yh, x, low:high] = part[:, tokens:].astype(BF16)


def project(pos, a, b, buffers, head, acc=()):
    tokens = a.shape[1]
    anywhere, vmem = (pl.BlockSpec(memory_space=space) for space in (pl.ANY, pltpu.VMEM))
    if head == 0:
        shapes, out_specs = pltpu.HBM((2, 4, 192, 2 * tokens), F32), vmem
    else:
        shapes = [jax.ShapeDtypeStruct((2, 4, 192, tokens), BF16)] * 2
        out_specs = [vmem, vmem]
    return pl.pallas_call(
        functools.partial(project_kernel, head),
        grid_spec=pltpu.PrefetchScalarGridSpec(
            num_scalar_prefetch=1,
            grid=(1,),
            in_specs=[anywhere] * 2 + [vmem] * (len(buffers) + len(acc)),
            out_specs=out_specs,
            scratch_shapes=[
                pltpu.VMEM((2, *a.shape), BF16),
                pltpu.VMEM((2 * tokens, 16 * HEAD_DIM), BF16),
                pltpu.SemaphoreType.DMA((2,)),
            ],
        ),
        out_shape=shapes,
        compiler_params=pltpu.CompilerParams(vmem_limit_bytes=24 << 20),
        cost_estimate=cost(2 * 256 * 2048 * 1536, 9 << 20),
    )(pos, a, b, *buffers, *acc)


def finish_kernel(pos_ref, mine_ref, other_ref, out_ref, mine, other, stack, sem):
    core = pos_ref[4]
    copies = [
        pltpu.make_async_copy(source, target, sem.at[i])
        for i, (source, target) in enumerate(((mine_ref, mine), (other_ref, other)))
    ]
    for copy in copies:
        copy.start()
    for copy in copies:
        copy.wait()
    for yh in range(2):
        for x in range(4):
            block = stack.at[yh * 4 + x]
            block[pl.ds(pl.multiple_of(core * 192, 64), 192)] = mine[yh, x]
            block[pl.ds(pl.multiple_of((1 - core) * 192, 64), 192)] = other[yh, x]
            low = (yh * 4 + x) * 384
            out_ref[:, low : low + 384] = block[...].T


def finish(pos, mine, other):
    tokens = mine.shape[3]
    anywhere = pl.BlockSpec(memory_space=pl.ANY)
    return pl.pallas_call(
        finish_kernel,
        grid_spec=pltpu.PrefetchScalarGridSpec(
            num_scalar_prefetch=1,
            grid=(1,),
            in_specs=[anywhere, anywhere],
            out_specs=pl.BlockSpec((tokens, 3072), lambda i, p: (0, 0)),
            scratch_shapes=[
                pltpu.VMEM(mine.shape, BF16),
                pltpu.VMEM(mine.shape, BF16),
                pltpu.VMEM((8, 384, tokens), BF16),
                pltpu.SemaphoreType.DMA((2,)),
            ],
        ),
        out_shape=jax.ShapeDtypeStruct((tokens, 3072), BF16),
        compiler_params=pltpu.CompilerParams(vmem_limit_bytes=8 << 20),
        cost_estimate=cost(0, 2 << 20),
        name="finish",
    )(pos, mine, other)


def shift(value, axis, size, step):
    return lax.ppermute(value, axis, [(i, (i + step) % size) for i in range(size)])


def pair_swap(value):
    return lax.ppermute(value, "yl", [(0, 1), (1, 0)])


def cross_swap(value):
    return lax.ppermute(value, ("yh", "yl"), [(1, 2), (2, 1), (3, 0), (0, 3)])


def core_swap(value):
    return lax.ppermute(value, "core", [(0, 1), (1, 0)])


def split_kernel(*refs):
    *blocks, a_ref, b_ref = refs
    for i, block in enumerate(blocks):
        for head in range(2):
            lanes = slice(head * HEAD_DIM, (head + 1) * HEAD_DIM)
            a_ref[i, head] = block[:ROWS_A, lanes]
            b_ref[i, head] = block[ROWS_A:, lanes]


def split_rows(blocks):
    return pl.pallas_call(
        split_kernel,
        out_shape=[
            jax.ShapeDtypeStruct((len(blocks), 2, rows, HEAD_DIM), BF16) for rows in (ROWS_A, ROWS_B)
        ],
        compiler_params=pltpu.CompilerParams(vmem_limit_bytes=8 << 20),
        cost_estimate=cost(0, 1 << 20),
    )(*blocks)


def spread(blocks):
    a, b = split_rows(blocks)
    b_pair, b_cross = pair_swap(b), cross_swap(b)
    a_up, a_down = shift(a, "x", 4, 1), shift(a, "x", 4, -1)
    b_far, a_up2 = cross_swap(b_pair), shift(a_up, "x", 4, 1)
    near = jnp.stack([b, b_pair])
    a, far = jnp.stack([a, a_up, a_down, a_up2]), jnp.stack([b_cross, b_far])
    up, down = [shift(near, "x", 4, 1)], [shift(near, "x", 4, -1)]
    a_pair, a_cross = pair_swap(a), cross_swap(a)
    up.append(shift(far, "x", 4, 1))
    down.append(shift(far, "x", 4, -1))
    up_last = shift(up[0], "x", 4, 1)
    a_far = cross_swap(a_pair)
    last = [up_last, shift(down[1], "x", 4, -1)]
    return (a, a_pair, a_cross, a_far, near, far, *up, *down, *last)


def all_to_all(value):
    return lax.all_to_all(value, SEQ, 0, 0, tiled=True)


def per_device(queries, key_rows, value_rows, w_out):
    q, k, v = queries[0], key_rows[0], value_rows[0]
    pos = jnp.stack([lax.axis_index(n) for n in ("yh", "yl", "z", "x", "core")]).astype(jnp.int32)
    wt = w_out.T

    near = {step: shift(wt, "z", 8, -step) for step in NEAR[1:]}
    packed0 = pack(q, k, v, 0)
    sent0 = all_to_all(packed0)
    far = {
        -3: shift(near[-2], "z", 8, 1),
        3: shift(near[2], "z", 8, -1),
        -4: shift(near[-2], "z", 8, 2),
    }
    weights = spread([wt] + [near[step] for step in NEAR[1:]] + [far[step] for step in FAR])

    packed1 = pack(q, k, v, 1)
    sent1 = all_to_all(packed1)
    mixed0 = attend(sent0)
    back0 = all_to_all(mixed0)
    mixed1 = attend(sent1)
    back1 = all_to_all(mixed1)
    other0 = core_swap(back0)
    rows0 = load(back0, weights, 0)
    acc = project(pos, back0, other0, rows0, 0)
    other1 = core_swap(back1)
    rows1 = load(back1, weights, 1)
    mine, theirs = project(pos, back1, other1, rows1, 1, (acc,))
    return finish(pos, mine, core_swap(theirs))[None]


def solution(mesh):
    fine = Mesh(mesh.devices.reshape(2, 4, 2, 2, 8), DP + SEQ)
    rows = P(DP, SEQ, None)
    return jax.shard_map(
        per_device,
        mesh=fine,
        in_specs=(rows, rows, rows, P(SEQ, DP)),
        out_specs=rows,
        check_vma=False,
    )
```
